256 devices in a mesh: gr: 16 (over z, core), gc: 16 (over x, y).
Axes of the slice: x: 4, y: 4, z: 8, core: 2. Of those that a mesh axis runs over, the one named last changes fastest.
Arguments:
- out_grad: bfloat16 [131072, 512], P(('gr', 'gc')), may hold values from -6 to 6
- preactivation_state: bfloat16 [131072, 512], P(('gr', 'gc')), may hold values from -6 to 6
- features: bfloat16 [131072, 512], P(('gc', 'gr')), may hold values from -24 to 24
- weight: bfloat16 [512, 512], replicated, may hold values from -0.25 to 0.25
- block_values: bfloat16 [16, 16, 152, 128, 128], P('gr', 'gc'), may hold values from -0.1875 to 0.1875
- block_rows: int32 [16, 16, 152], P('gr', 'gc'), may hold values from 0 to 63, as said below
- block_cols: int32 [16, 16, 152], P('gr', 'gc'), may hold values from 0 to 63, as said below
- block_counts: int32 [16, 16], P('gr', 'gc'), may hold values from 1 to 152, as said below
Outputs:
- input_grad: bfloat16 [131072, 512], P(('gc', 'gr'))
- weight_grad: float32 [512, 512], replicated
The draws below stay inside these ranges and needn't reach their ends.
Inputs may be any that keep to these rules, and one draw needn't show every extreme that they name: `block_rows`: block row within a tile; some entry equals 63. `block_cols`: block column within a tile; some entry equals 63. `block_counts`: slots from this count on are unused; some tile uses all 152 slots.
All inputs are finite; a program needn't handle non-finite values.
Results may differ from the reference program's by a relative error of at most 0.014.
Values may be sent and summed in bfloat16 or wider, within the bound.
A program may use at most 128 MiB of HBM per device.

```python
import jax
import jax.numpy as jnp
from jax import lax

D = 512
BLOCK = 128
ROWS_DEV = 512
BMAX = 152
NODES = 131072
ROW_BLOCKS = 64
COL_BLOCKS = 64
N_GR = 16
N_GC = 16


def draw_block_counts(key, part):
    first, second, third = jax.random.split(jax.random.fold_in(key, 11), 3)
    left = jax.random.randint(first, (N_GR, N_GC), 1, BMAX + 1)
    right = jax.random.randint(second, (N_GR, N_GC), 1, BMAX + 1)
    counts = (left * right + BMAX - 1) // BMAX
    peak = jax.random.randint(third, (), 0, N_GR * N_GC)
    places = jnp.arange(N_GR * N_GC).reshape(N_GR, N_GC)
    return jnp.where(places == peak, BMAX, counts).astype(jnp.int32)


def draw_block_rows(key, part):
    picks = jax.random.randint(jax.random.fold_in(key, 12), (N_GR, N_GC, BMAX), 0, ROW_BLOCKS)
    return picks.at[0, 0, 0].set(ROW_BLOCKS - 1).astype(jnp.int32)


def draw_block_cols(key, part):
    picks = jax.random.randint(jax.random.fold_in(key, 13), (N_GR, N_GC, BMAX), 0, COL_BLOCKS)
    return picks.at[0, 0, 0].set(COL_BLOCKS - 1).astype(jnp.int32)


def strengthened(array, own_key, source, target, parts, factor):
    def block_of(axis_at):
        return (jnp.arange(array.shape[axis_at]) // (array.shape[axis_at] // parts)).reshape((-1,) + (1,) * (array.ndim - 1 - axis_at))

    near = jax.random.permutation(own_key, parts)[block_of(target)]
    far = (block_of(target) + parts // 2) % parts
    return jnp.where((block_of(source) == near) | (block_of(source) == far), factor * array, array)


def block_scale(key, extent, cuts, smallest, largest):
    level, own = 1.0, jax.random.fold_in(key, 6)
    for position, shards_of in cuts:
        steps = jnp.exp(jax.random.uniform(jax.random.fold_in(own, position), (shards_of,), jnp.float32, smallest / len(cuts), largest / len(cuts)))
        level = level * jnp.repeat(steps, extent[position] // shards_of).reshape([-1 if axis == position else 1 for axis in range(len(extent))])
    return level


def scatter_about(key, shape, deviation, reach, pieces=(), held_as=jnp.bfloat16):
    result = deviation * jax.random.normal(key, shape, jnp.float32)
    if pieces:
        result = result * block_scale(key, shape, pieces, -0.22, 0.18)
    return jnp.clip(result, -reach, reach).astype(held_as)


def gaussian_with(key, dims, scale, bound, cuts, heavy, kind=jnp.bfloat16):
    drawn = scale * jax.random.normal(key, dims, jnp.float32)
    if cuts:
        drawn = drawn * block_scale(key, dims, cuts, -0.22, 0.18)
    return jnp.clip(strengthened(drawn, jax.random.fold_in(key, 3), *heavy), -bound, bound).astype(kind)


def setup_inputs(seed: int = 0) -> dict:
    arg_keys = jax.random.split(jax.random.key(seed), 9)
    out_grad = scatter_about(arg_keys[0], (NODES, D), 1.0, 6.0, ((0, 256),))
    preactivation_state = scatter_about(arg_keys[1], (NODES, D), 1.0, 6.0, ((0, 256),))
    features = gaussian_with(arg_keys[2], (NODES, D), 1.0, 24.0, ((0, 256),), (0, 1, 256, 6.0))
    weight = scatter_about(arg_keys[3], (D, D), D ** -0.5, 0.25)
    block_values = scatter_about(arg_keys[4], (N_GR, N_GC, BMAX, BLOCK, BLOCK), (BLOCK * 8) ** -0.5, 0.1875, ((0, 16), (1, 16)))
    block_rows = draw_block_rows(jax.random.fold_in(arg_keys[8], 71), 0)
    block_cols = draw_block_cols(jax.random.fold_in(arg_keys[8], 71), 0)
    block_counts = draw_block_counts(jax.random.fold_in(arg_keys[8], 71), 0)
    return {"out_grad": out_grad, "preactivation_state": preactivation_state, "features": features, "weight": weight, "block_values": block_values, "block_rows": block_rows, "block_cols": block_cols, "block_counts": block_counts}


def tile_partial(masked, block_values, block_rows, block_cols, block_counts, tile_row, tile_col):
    tile_height = ROWS_DEV * N_GC
    offset = (tile_row * tile_height).astype(jnp.int32)
    rows_now = lax.dynamic_slice_in_dim(masked, offset, tile_height, 0).reshape(ROW_BLOCKS, BLOCK, D)
    current_values = block_values[tile_row, tile_col]
    selected_entries = rows_now[block_rows[tile_row, tile_col]]
    contribution = jnp.einsum('yql,yqa->yla', current_values.astype(jnp.float32), selected_entries.astype(jnp.float32))
    active = jnp.arange(BMAX) < block_counts[tile_row, tile_col]
    contribution = jnp.where(active[:, None, None], contribution, jnp.zeros_like(contribution))
    value_partial_sum = jnp.zeros((COL_BLOCKS, BLOCK, D), jnp.float32).at[block_cols[tile_row, tile_col]].add(contribution)
    return value_partial_sum.reshape(COL_BLOCKS * BLOCK, D).astype(jnp.bfloat16)


def reference(out_grad, preactivation_state, features, weight, block_values, block_rows, block_cols, block_counts):
    masked = jnp.where(preactivation_state > 0, out_grad, jnp.zeros_like(out_grad)).astype(jnp.bfloat16)

    def column_sum(tile_col):
        def add_tile(tile_row, total):
            return total + tile_partial(masked, block_values, block_rows, block_cols, block_counts, tile_row, tile_col).astype(jnp.float32)
        return lax.fori_loop(0, N_GR, add_tile, jnp.zeros((ROWS_DEV * N_GR, D), jnp.float32))

    totals = lax.map(column_sum, jnp.arange(N_GC, dtype=jnp.int32))
    spread = totals.reshape(NODES, D).astype(jnp.bfloat16)
    input_grad = jnp.dot(spread, weight.T, preferred_element_type=jnp.float32).astype(jnp.bfloat16)
    weight_grad = jnp.dot(features.T, spread, preferred_element_type=jnp.float32) * (NODES ** -0.5)
    return input_grad, weight_grad
```

```python
import functools

import jax
import jax.numpy as jnp
from jax import lax
from jax.experimental import pallas as pl
from jax.experimental.pallas import tpu as pltpu
from jax.sharding import PartitionSpec as P

MESH = pl.DeviceIdType.MESH
F32, BF16 = jnp.float32, jnp.bfloat16
NX, NY, NZ = 4, 4, 8
NXY = NX * NY
BLOCK = 128
BPD = 4
CHUNKS = 4
UNROLL = 4
GROUPS = ((0, 1, 2), (3,))


def gather_messages():
    table = {}

    def add(key, axis, sign, owner, first, count):
        table[key] = (len(table), axis, sign, owner, first, count)

    for h in (0, 1):
        first = 2 * h

        def at(u, v):
            return (u, v) if h == 0 else (v, u)

        u_axis, v_axis = (0, 1) if h == 0 else (1, 0)
        add((h, "m1", 1), u_axis, 1, at(0, 0), first, 2)
        add((h, "m1", -1), u_axis, -1, at(0, 0), first, 2)
        add((h, "m2", 1), u_axis, 1, at(-1, 0), first, 1)
        add((h, "m2", -1), u_axis, -1, at(1, 0), first + 1, 1)
        for j in (0, -1, 1, 2):
            add((h, "n1", 1, j), v_axis, 1, at(j, 0), first, 2)
            add((h, "n1", -1, j), v_axis, -1, at(j, 0), first, 2)
            add((h, "n2", 1, j), v_axis, 1, at(j, -1), first, 1)
            add((h, "n2", -1, j), v_axis, -1, at(j, 1), first + 1, 1)
    return table


GATHER = gather_messages()


def kernel(slots, aux, og, state, feat, w, vals, ig, wg,
           xt, a, r, pp, sib, cs, cr, st, ft, bufs, sems):
    gr, gc = lax.axis_index("gr"), lax.axis_index("gc")
    z, core = lax.div(gr, 2), lax.rem(gr, 2)
    x, y = lax.div(gc, NY), lax.rem(gc, NY)
    dc = xt[0].shape[1]
    gsend, grecv, psend, precv, csend, crecv, vsem, wsems = sems
    pending = []

    def mesh_at(dx=0, dy=0, dz=0, other=False):
        c = 1 - core if other else core
        return {
            "gr": lax.rem(z + dz + NZ, NZ) * 2 + c,
            "gc": lax.rem(x + dx + NX, NX) * NY + lax.rem(y + dy + NY, NY),
        }

    def xy_peer(i):
        return {"gr": gr, "gc": lax.rem(gc + i, NXY)}

    def remote(src, dst, send, recv, device):
        return pltpu.make_async_remote_copy(
            src_ref=src, dst_ref=dst, send_sem=send, recv_sem=recv,
            device_id=device, device_id_type=MESH)

    def start(copy):
        copy.start()
        pending.append(copy)

    def gmsg(k, key):
        index, axis, sign, (ox, oy), first, count = GATHER[key]
        owner = lax.rem(x + ox + NX, NX) * NY + lax.rem(y + oy + NY, NY)
        ref = xt[k].at[pl.ds(owner * BPD + first, count)]
        device = mesh_at(dx=sign) if axis == 0 else mesh_at(dy=sign)
        return remote(ref, ref, gsend.at[k, index], grecv.at[k, index], device)

    def mask(k):
        for b in range(BPD):
            rows, cols = slice(b * BLOCK, (b + 1) * BLOCK), slice(k * dc, (k + 1) * dc)
            kept = jnp.where(state[rows, cols] > 0, og[rows, cols], jnp.zeros((BLOCK, dc), BF16))
            xt[k][gc * BPD + b] = kept.T

    def e0(k):
        for h in (0, 1):
            for sign in (1, -1):
                start(gmsg(k, (h, "m1", sign)))
        for h in (0, 1):
            for sign in (1, -1):
                start(gmsg(k, (h, "n1", sign, 0)))

    def e1(k):
        for h in (0, 1):
            for sign in (1, -1):
                gmsg(k, (h, "m1", sign)).wait_recv()
                start(gmsg(k, (h, "m2", sign)))
                start(gmsg(k, (h, "n1", 1, -sign)))
                start(gmsg(k, (h, "n1", -1, -sign)))
        for h in (0, 1):
            for sign in (1, -1):
                gmsg(k, (h, "n1", sign, 0)).wait_recv()
                start(gmsg(k, (h, "n2", sign, 0)))

    def e2(k):
        for h in (0, 1):
            gmsg(k, (h, "m2", 1)).wait_recv()
            gmsg(k, (h, "m2", -1)).wait_recv()
            start(gmsg(k, (h, "n1", 1, 2)))
            start(gmsg(k, (h, "n1", -1, 2)))
        for j in (-1, 1):
            for h in (0, 1):
                for sign in (1, -1):
                    gmsg(k, (h, "n1", sign, j)).wait_recv()
                    start(gmsg(k, (h, "n2", sign, j)))

    def e3(k):
        for h in (0, 1):
            for sign in (1, -1):
                gmsg(k, (h, "n1", sign, 2)).wait_recv()
                start(gmsg(k, (h, "n2", sign, 2)))

    def e4(k):
        for j in (0, -1, 1, 2):
            for h in (0, 1):
                for sign in (1, -1):
                    gmsg(k, (h, "n2", sign, j)).wait_recv()

    def product(k, low, high):
        def step(i, carry):
            s = i * UNROLL
            terms = [jnp.dot(xt[k][aux[s + t]], a[s + t], preferred_element_type=F32) for t in range(UNROLL)]
            for t in range(UNROLL):
                r[s + 1 + t] = r[aux[slots + s + t]] + terms[t]
            return carry

        lax.fori_loop(low, high, step, 0)

    def collect(k, c):
        def step(i, carry):
            for b in range(BPD):
                pp[k, c, i, b] = r[aux[2 * slots + (i * 2 + c) * BPD + b]].astype(BF16)
            return carry

        lax.fori_loop(0, NZ, step, 0)

    def pair_copy(k):
        return remote(pp.at[k, 1 - core], sib.at[k], psend.at[k], precv.at[k], mesh_at(other=True))

    def chain_copy(k, d, s):
        part = pl.ds(2 * d, 2) if s == 0 else pl.ds(0, BPD)
        return remote(cs.at[k, d, s, part], cr.at[k, d, s, part], csend.at[k, d, s], crecv.at[k, d, s],
                      mesh_at(dz=1 if d == 0 else -1))

    def chain(k, s):
        if s == 0:
            pair_copy(k).wait_recv()
        for d in (0, 1):
            far = NZ // 2 - s
            target = lax.rem(z + (far if d == 0 else NZ - far), NZ)
            if s > 0:
                chain_copy(k, d, s - 1).wait_recv()
            half = (2 * d, 2 * d + 1)
            for b in half if s == 0 else range(BPD):
                total = pp[k, core, target, b].astype(F32) + sib[k, target, b].astype(F32)
                if s > 1 or (s == 1 and b in half):
                    total = total + cr[k, d, s - 1, b].astype(F32)
                cs[k, d, s, b] = total.astype(BF16)
            start(chain_copy(k, d, s))

    def settle(k):
        for d in (0, 1):
            chain_copy(k, d, 3).wait_recv()
        for b in range(BPD):
            total = pp[k, core, z, b].astype(F32) + sib[k, z, b].astype(F32)
            total = total + cr[k, 0, 3, b].astype(F32) + cr[k, 1, 3, b].astype(F32)
            st[k * dc:(k + 1) * dc, b * BLOCK:(b + 1) * BLOCK] = total.astype(BF16)
        term = lax.dot_general(ft[...], st[k * dc:(k + 1) * dc, :], (((1,), (1,)), ((), ())),
                               preferred_element_type=F32)
        for n, group in enumerate(GROUPS):
            if k in group:
                bufs[n][0][:, :, group.index(k)] = term.astype(BF16).reshape(2, NXY, 16, dc)

    def wmsg(n, kind, i=0):
        own, fromsib, mine, got, zgot, out = bufs[n]
        s_send, s_recv = wsems[n]
        if kind == "pair":
            return remote(own.at[1 - core], fromsib, s_send.at[0], s_recv.at[0], mesh_at(other=True))
        if kind == "xy":
            return remote(mine.at[lax.rem(gc + i, NXY)], got.at[gc], s_send.at[i], s_recv.at[i], xy_peer(i))
        if kind == "z":
            return remote(zgot.at[z], zgot.at[z], s_send.at[NXY + i], s_recv.at[NXY + i], mesh_at(dz=i))
        if kind == "back":
            return remote(out.at[core, gc], out.at[core, gc], s_send.at[NXY + NZ + i], s_recv.at[NXY + NZ + i],
                          xy_peer(i))
        return remote(out.at[core], out.at[core], s_send.at[NXY + NZ], s_recv.at[NXY + NZ], mesh_at(other=True))

    def w0(n):
        start(wmsg(n, "pair"))

    def w1(n):
        own, fromsib, mine, got, zgot, out = bufs[n]
        wmsg(n, "pair").wait_recv()
        mine[...] = (own[core].astype(F32) + fromsib[...].astype(F32)).astype(BF16)
        for i in range(1, NXY):
            start(wmsg(n, "xy", i))
        got[gc] = mine[gc]

    def w2(n):
        own, fromsib, mine, got, zgot, out = bufs[n]
        for i in range(1, NXY):
            wmsg(n, "xy", i).wait_recv()
        total = got[0].astype(F32)
        for q in range(1, NXY):
            total = total + got[q].astype(F32)
        zgot[z] = total.astype(zgot.dtype)
        for i in range(1, NZ):
            start(wmsg(n, "z", i))

    def w3(n):
        own, fromsib, mine, got, zgot, out = bufs[n]
        for i in range(1, NZ):
            wmsg(n, "z", i).wait_recv()
        total = zgot[0].astype(F32)
        for q in range(1, NZ):
            total = total + zgot[q].astype(F32)
        out[core, gc] = total.astype(out.dtype)
        for i in range(1, NXY):
            start(wmsg(n, "back", i))

    def w4(n):
        for i in range(1, NXY):
            wmsg(n, "back", i).wait_recv()
        start(wmsg(n, "last"))

    def w5(n):
        out = bufs[n][5]
        wmsg(n, "last").wait_recv()
        for g, k in enumerate(GROUPS[n]):
            wg[:, k * dc:(k + 1) * dc] = out[:, :, g].astype(F32).reshape(2 * NXY * 16, dc)

    load = pltpu.make_async_copy(vals, a, vsem)
    load.start()
    barrier = pltpu.get_barrier_semaphore()
    partners = [mesh_at(other=True)] + [mesh_at(dz=i) for i in range(1, NZ)] + [xy_peer(i) for i in range(1, NXY)]
    for device in partners:
        pl.semaphore_signal(barrier, inc=1, device_id=device, device_id_type=MESH)
    mask(0)
    pl.semaphore_wait(barrier, len(partners))
    e0(0)
    mask(1)
    e1(0)
    for k in range(2, CHUNKS):
        mask(k)
    e2(0)
    e0(1)
    ft[...] = feat[...].T
    r[0] = jnp.zeros(r.shape[1:], F32)
    e3(0)
    load.wait()
    e4(0)
    total_steps = slots // UNROLL
    pieces = 6
    cut = [total_steps * i // pieces for i in range(pieces + 1)]
    for k in range(CHUNKS):
        more = k + 1 < CHUNKS
        back = k > 0
        for i in range(pieces):
            product(k, cut[i], cut[i + 1])
            if i == 0:
                if back:
                    chain(k - 1, 1)
                if more:
                    e1(k + 1)
            if i == 1 and back:
                chain(k - 1, 2)
            if i == 2 and more:
                e2(k + 1)
                if k + 2 < CHUNKS:
                    e0(k + 2)
            if i == 3:
                if back:
                    chain(k - 1, 3)
                if more:
                    e3(k + 1)
            if i == 4 and back:
                settle(k - 1)
        collect(k, 1 - core)
        start(pair_copy(k))
        collect(k, core)
        if k == CHUNKS - 1:
            w0(0)
        chain(k, 0)
        if more:
            e4(k + 1)
    last = CHUNKS - 1
    chain(last, 1)
    w1(0)
    chain(last, 2)
    chain(last, 3)
    w2(0)
    settle(last)
    w0(1)
    w3(0)
    w1(1)
    ig[...] = lax.dot_general(st[...], w[...], (((0,), (1,)), ((), ())), preferred_element_type=F32).astype(BF16)
    w4(0)
    w2(1)
    w5(0)
    w3(1)
    w4(1)
    w5(1)
    for copy in pending:
        copy.wait_send()


def local(og, state, feat, w, vals, rows, cols, counts):
    slots = vals.shape[2]
    width = og.shape[1]
    dc = width // CHUNKS
    rows, cols, count = rows[0, 0], cols[0, 0], counts[0, 0]
    place = jnp.arange(slots, dtype=jnp.int32)
    columns = jnp.arange(BPD * NZ * 2, dtype=jnp.int32)
    wanted = jnp.concatenate([cols, columns])
    limit = jnp.concatenate([jnp.minimum(place, count), jnp.full_like(columns, count)])
    hit = (wanted[:, None] == cols[None, :]) & (place[None, :] < limit[:, None])
    latest = jnp.max(jnp.where(hit, place[None, :] + 1, 0), axis=1)
    aux = jnp.concatenate([rows, latest])

    def group_bufs(n):
        g = len(GROUPS[n])
        return (
            pltpu.VMEM((2, NXY, g, 16, dc), BF16),
            pltpu.VMEM((NXY, g, 16, dc), BF16),
            pltpu.VMEM((NXY, g, 16, dc), BF16),
            pltpu.VMEM((NXY, g, 16, dc), BF16),
            pltpu.VMEM((NZ, g, 16, dc), F32),
            pltpu.VMEM((2, NXY, g, 16, dc), BF16),
        )

    nm = len(GATHER)
    dma = pltpu.SemaphoreType.DMA
    ww = 2 * NXY + NZ
    vm = pl.BlockSpec(memory_space=pltpu.VMEM)
    ig, wg = pl.pallas_call(
        functools.partial(kernel, slots),
        out_shape=(jax.ShapeDtypeStruct((og.shape[0], w.shape[0]), BF16),
                   jax.ShapeDtypeStruct((feat.shape[1], width), F32)),
        in_specs=[pl.BlockSpec(memory_space=pltpu.SMEM), vm, vm, vm, vm, pl.BlockSpec(memory_space=pl.ANY)],
        out_specs=(vm, vm),
        scratch_shapes=[
            tuple(pltpu.VMEM((BPD * NXY, dc, BLOCK), BF16) for _ in range(CHUNKS)),
            pltpu.VMEM((slots, BLOCK, BLOCK), BF16),
            pltpu.VMEM((slots + 1, dc, BLOCK), F32),
            pltpu.VMEM((CHUNKS, 2, NZ, BPD, dc, BLOCK), BF16),
            pltpu.VMEM((CHUNKS, NZ, BPD, dc, BLOCK), BF16),
            pltpu.VMEM((CHUNKS, 2, 4, BPD, dc, BLOCK), BF16),
            pltpu.VMEM((CHUNKS, 2, 4, BPD, dc, BLOCK), BF16),
            pltpu.VMEM((width, og.shape[0]), BF16),
            pltpu.VMEM((feat.shape[1], feat.shape[0]), BF16),
            tuple(group_bufs(n) for n in range(len(GROUPS))),
            (dma((CHUNKS, nm)), dma((CHUNKS, nm)), dma((CHUNKS,)), dma((CHUNKS,)),
             dma((CHUNKS, 2, 4)), dma((CHUNKS, 2, 4)), dma,
             tuple((dma((ww,)), dma((ww,))) for _ in GROUPS)),
        ],
        compiler_params=pltpu.CompilerParams(
            collective_id=0, has_side_effects=True, vmem_limit_bytes=67043328),
    )(aux, og, state, feat, w, vals.reshape(vals.shape[2:]))
    nodes = og.shape[0] * lax.axis_size("gr") * lax.axis_size("gc")
    return ig, wg * (nodes ** -0.5)


def solution(mesh):
    in_specs = (
        P(("gr", "gc"), None),
        P(("gr", "gc"), None),
        P(("gc", "gr"), None),
        P(),
        P("gr", "gc", None, None, None),
        P("gr", "gc", None),
        P("gr", "gc", None),
        P("gr", "gc"),
    )
    out_specs = (P(("gc", "gr"), None), P())
    return jax.shard_map(local, mesh=mesh, in_specs=in_specs, out_specs=out_specs, check_vma=False)
```
